256 devices in a mesh: row: 32 (over y, z), col: 8 (over x, core).
Axes of the slice: x: 4, y: 4, z: 8, core: 2. Of those that a mesh axis runs over, the one named last changes fastest.
Arguments:
- trailing_matrix: float32 [8192, 8192], P('row', 'col'), may hold values from -24 to 1024, as said below
- rhs_block: float32 [8192, 128], P('row'), may hold values from -144 to 144
Outputs:
- factored: float32 [8192, 8192], P('row', 'col')
- solved_rhs: float32 [8192, 128], P('row')
The draws below stay inside these ranges and needn't reach their ends.
Inputs may be any that keep to these rules, and one draw needn't show every extreme that they name: `trailing_matrix`: symmetric in logical order; its leading 2 * 256 by 512 logical block is positive definite.
All inputs are finite; a program needn't handle non-finite values.
Results may differ from the reference program's by a relative error of at most 0.00011.
Values sent between devices are 32-bit elements; how exact they have to be, the bound alone decides.
No kernel may reach another device: no remote copies, remote signals or barrier semaphores. Data moves between devices by JAX's collectives and lax.ppermute only.
A program may use at most 64 MiB of HBM per device.

```python
import jax
import jax.numpy as jnp
from jax import lax

NB = 256
NR = 128
TROW = 1
TCOL = 4
M = 8192
N_ROW = 32
N_COL = 8


def stored_logical(total_len, tiles_dev, parts_count):
    stored = jnp.arange(total_len, dtype=jnp.int32)
    tile_pos = stored // NB
    return (tile_pos // tiles_dev + parts_count * (tile_pos % tiles_dev)) * NB + stored % NB


def draw_trailing_matrix(key, part):
    keys = jax.random.split(key, 3)
    lead_len = 2 * NB
    index_all = jnp.arange(M, dtype=jnp.int32)
    noise = jnp.clip(jax.random.normal(keys[0], (M, M), jnp.float32), -6.0, 6.0)
    upper = index_all[:, None] <= index_all[None, :]
    noise = jnp.where(upper, noise, noise.T)
    in_lead = index_all < lead_len
    boxed = jax.random.uniform(keys[1], (M, M), jnp.float32, -1.0, 1.0)
    boxed = jnp.where(upper, boxed, boxed.T)
    diag_vals = lead_len * (1.0 + jax.random.uniform(keys[2], (M,), jnp.float32, 0.1, 1.0))
    edge = in_lead[:, None] != in_lead[None, :]
    outer = jnp.clip(noise * jnp.where(edge, 4.0, 1.0), -24.0, 24.0)
    both_lead = in_lead[:, None] & in_lead[None, :]
    logical = jnp.where(both_lead, boxed, outer)
    on_diag = (index_all[:, None] == index_all[None, :]) & both_lead
    logical = jnp.where(on_diag, diag_vals[:, None], logical)
    rows_map = stored_logical(M, TROW, N_ROW)
    cols_map = stored_logical(M, TCOL, N_COL)
    return jnp.take(jnp.take(logical, rows_map, axis=0), cols_map, axis=1)


def draw_rhs_block(key, part):
    index_all = jnp.arange(M, dtype=jnp.int32)
    noise = jnp.clip(jax.random.normal(key, (M, NR), jnp.float32), -6.0, 6.0)
    row_scale = jnp.where(index_all < 2 * NB, 24.0, 1.0)
    logical = noise * row_scale[:, None]
    rows_map = stored_logical(M, TROW, N_ROW)
    return jnp.take(logical, rows_map, axis=0)


def setup_inputs(seed: int = 0) -> dict:
    key_list = jax.random.split(jax.random.key(seed), 3)
    return {
        "trailing_matrix": draw_trailing_matrix(jax.random.fold_in(key_list[2], 71), 0),
        "rhs_block": draw_rhs_block(jax.random.fold_in(key_list[2], 71), 0),
    }


def logical_to_stored(total_len, tiles_dev, parts_count):
    logical = jnp.arange(total_len, dtype=jnp.int32)
    tile_pos = logical // NB
    return (tile_pos % parts_count * tiles_dev + tile_pos // parts_count) * NB + logical % NB

def stored_to_logical(total_len, tiles_dev, parts_count):
    stored = jnp.arange(total_len, dtype=jnp.int32)
    tile_pos = stored // NB
    return (tile_pos // tiles_dev + parts_count * (tile_pos % tiles_dev)) * NB + stored % NB

def reference(trailing_matrix, rhs_block):
    highest = lax.Precision.HIGHEST
    row_take = logical_to_stored(M, TROW, N_ROW)
    col_take = logical_to_stored(M, TCOL, N_COL)
    work = jnp.take(jnp.take(trailing_matrix, row_take, axis=0), col_take, axis=1)
    right = jnp.take(rhs_block, row_take, axis=0)
    result = jnp.zeros_like(work)
    for section in range(2):
        start_pos = section * NB
        end_pos = start_pos + NB
        factor = jnp.linalg.cholesky(work[start_pos:end_pos, start_pos:end_pos])
        below_rows = jax.scipy.linalg.solve_triangular(factor, work[end_pos:, start_pos:end_pos].T, lower=True).T
        solved = jax.scipy.linalg.solve_triangular(factor, right[start_pos:end_pos], lower=True)
        right = right.at[start_pos:end_pos].set(solved)
        right = right.at[end_pos:].set(right[end_pos:] - jnp.dot(below_rows, solved, precision=highest))
        work = work.at[end_pos:, end_pos:].set(work[end_pos:, end_pos:] - jnp.dot(below_rows, below_rows.T, precision=highest))
        result = result.at[start_pos:end_pos, start_pos:end_pos].set(factor)
        result = result.at[end_pos:, start_pos:end_pos].set(below_rows)
    result = result.at[2 * NB:, 2 * NB:].set(work[2 * NB:, 2 * NB:])
    row_back = stored_to_logical(M, TROW, N_ROW)
    col_back = stored_to_logical(M, TCOL, N_COL)
    factored = jnp.take(jnp.take(result, row_back, axis=0), col_back, axis=1)
    solved_rhs = jnp.take(right, row_back, axis=0)
    return (factored, solved_rhs)
```

```python
import jax
import jax.numpy as jnp
from jax import lax
from jax.experimental import pallas as pl
from jax.experimental.pallas import tpu as pltpu
from jax.sharding import Mesh
from jax.sharding import PartitionSpec as P

NB = 256
BLK = 128
SUB = 8
AXES = ("y", "z", "x", "core")
NY, NZ, NX, NK = 4, 8, 4, 2


highest = lax.Precision.HIGHEST


def fid(y, z, x, k):
    return ((y % NY * NZ + z % NZ) * NX + x % NX) * NK + k


EVERY = [
    (y, z, x, k) for y in range(NY) for z in range(NZ) for x in range(NX) for k in range(NK)
]


def shift(dy=0, dz=0):
    return [(fid(*p), fid(p[0] + dy, p[1] + dz, p[2], p[3])) for p in EVERY]


SWAP = [(fid(y, z, x, k), fid(y, z, x, 1 - k)) for y, z, x, k in EVERY]

RING4 = [[(0, 1)], [(0, 3), (1, 2)]]
RING8 = [[(0, 1)], [(0, 6), (1, 3)], [(0, 7), (1, 2), (6, 5), (3, 4)]]
RINGS = {"y": RING4, "z": RING8, "x": RING4}
SIZES = {"y": NY, "z": NZ, "x": NX}


def tree_rounds(order, root, core):
    have = {"y": [0], "z": [0], "x": [0]}
    rounds = []
    for axis in order:
        for pairs in RINGS[axis]:
            other = [n for n in "yzx" if n != axis]
            round_pairs = []
            for src, dst in pairs:
                for u in have[other[0]]:
                    for v in have[other[1]]:
                        ends = []
                        for val in (src, dst):
                            at = {axis: val, other[0]: u, other[1]: v}
                            ends.append(fid(at["y"] + root[0], at["z"] + root[1], at["x"] + root[2], core))
                        round_pairs.append(tuple(ends))
            have[axis] = have[axis] + [dst for _, dst in pairs]
            rounds.append(round_pairs)
    return rounds


def both_planes(root):
    first = tree_rounds("xyz", root, 0)
    second = tree_rounds("zyx", root, 1)
    return [a + b for a, b in zip(first, second)]


def send(value, pairs):
    return lax.ppermute(value, AXES, pairs)


def eliminate(rows, inv):
    n = len(rows)
    sub = lax.broadcasted_iota(jnp.int32, (SUB, BLK), 0)
    upper, lower_inv = [], []
    for k in range(n):
        D, F = rows[k], inv[k]
        col = [jnp.broadcast_to(D[:, SUB * k + s : SUB * k + s + 1], (SUB, BLK)) for s in range(SUB)]
        recip, cross, d_row, f_row = [], {}, [], []
        scale = jnp.zeros((SUB, BLK), jnp.float32)
        for s in range(SUB):
            pivot = jnp.broadcast_to(col[s][s : s + 1, :], (SUB, BLK))
            recip.append(1.0 / pivot)
            scale = jnp.where(sub == s, lax.rsqrt(pivot), scale)
            mult = jnp.where(sub > s, col[s] * recip[s], 0.0)
            for t in range(s + 1, SUB):
                cross[s, t] = jnp.broadcast_to(col[t][s : s + 1, :], (SUB, BLK))
                col[t] = col[t] - mult * cross[s, t]
            d_row.append(jnp.broadcast_to(D[s : s + 1, :], (SUB, BLK)))
            f_row.append(jnp.broadcast_to(F[s : s + 1, :], (SUB, BLK)))
            if s < SUB - 1:
                D = D - mult * d_row[s]
                F = F - mult * f_row[s]
        upper.append(D * scale)
        lower_inv.append(F * scale)
        for i in range(k + 1, n):
            part = [
                jnp.broadcast_to(rows[i][:, SUB * k + s : SUB * k + s + 1], (SUB, BLK))
                for s in range(SUB)
            ]
            p, q = rows[i], inv[i]
            for s in range(SUB):
                mult = part[s] * recip[s]
                for t in range(s + 1, SUB):
                    part[t] = part[t] - mult * cross[s, t]
                p = p - mult * d_row[s]
                q = q - mult * f_row[s]
            rows[i], inv[i] = p, q
    return upper, lower_inv


def factor_kernel(a_ref, u_ref, l_ref):
    n = BLK // SUB
    rows = [a_ref[SUB * i : SUB * i + SUB, :] for i in range(n)]
    r = lax.broadcasted_iota(jnp.int32, (SUB, BLK), 0)
    c = lax.broadcasted_iota(jnp.int32, (SUB, BLK), 1)
    inv = [jnp.where(r + SUB * i == c, 1.0, 0.0).astype(jnp.float32) for i in range(n)]
    upper, lower_inv = eliminate(rows, inv)
    for i in range(n):
        u_ref[SUB * i : SUB * i + SUB, :] = jnp.where(c >= r + SUB * i, upper[i], 0.0)
        l_ref[SUB * i : SUB * i + SUB, :] = lower_inv[i]


def factor_block(block):
    shape = jax.ShapeDtypeStruct((BLK, BLK), jnp.float32)
    return pl.pallas_call(factor_kernel, out_shape=[shape, shape])(block)


def mm(a, b):
    return lax.dot_general(a, b, (((1,), (0,)), ((), ())), precision=highest)


def mm_t(a, b):
    return lax.dot_general(a, b, (((1,), (1,)), ((), ())), precision=highest)


def t_mm(a, b):
    return lax.dot_general(a, b, (((0,), (0,)), ((), ())), precision=highest)


def factor_tile(a, b, c):
    ua, la = factor_block(a)
    ub = mm(la, b)
    uc, lc = factor_block(c - t_mm(ub, ub))
    corner = -mm(lc, t_mm(ub, la))
    zero = jnp.zeros((BLK, BLK), jnp.float32)
    upper = jnp.concatenate(
        [jnp.concatenate([ua, ub], 1), jnp.concatenate([zero, uc], 1)], 0
    )
    lower_inv = jnp.concatenate(
        [jnp.concatenate([la, zero], 1), jnp.concatenate([corner, lc], 1)], 0
    )
    return upper, lower_inv


def per_device(a, b):
    y, z, x, core = (lax.axis_index(n) for n in AXES)
    row = y * NZ + z
    col = x * NK + core
    tile = a[:, :NB]

    def at(*where):
        return (y == where[0]) & (z == where[1]) & (x == where[2])

    with jax.named_scope("lead1"):
        stack = jnp.concatenate(
            [tile[:BLK, :BLK], tile[:BLK, BLK:], tile[BLK:, BLK:]], 0
        )
        half = 3 * BLK // 2
        other = send(stack[half:], [(fid(0, 0, 0, 0), fid(0, 0, 0, 1))])
        mine = jnp.where(at(0, 0, 0), jnp.where(core == 0, stack[:half], other), 0.0)
        for pairs in both_planes((0, 0, 0)):
            mine = mine + send(mine, pairs)
        other = send(mine, SWAP)
        lead = jnp.where(
            core == 0, jnp.concatenate([mine, other], 0), jnp.concatenate([other, mine], 0)
        )

    with jax.named_scope("lead2"):
        flat = jnp.concatenate([tile[:, :BLK], tile[:, BLK:]], 0)
        b_zero = send(b, [(fid(0, 0, 0, 1), fid(0, 1, 0, 1))])
        pack = jnp.concatenate([flat, jnp.where(core == 0, b, b_zero)], 0)
        pack = jnp.where(at(0, 1, 0), pack, 0.0)
        for pairs in both_planes((0, 1, 0)):
            pack = pack + send(pack, pairs)
        other = send(pack, SWAP)
        low = jnp.where(core == 0, pack, other)
        high = jnp.where(core == 0, other, pack)
        a10 = jnp.concatenate([low[:NB], low[NB : 2 * NB]], 1)
        a11 = jnp.concatenate([high[:NB], high[NB : 2 * NB]], 1)
        b1, b0 = low[2 * NB :], high[2 * NB :]

    with jax.named_scope("cols"):
        quarter = NB // 4
        piece = None
        for q in range(4):
            pairs = [
                (fid(yy, zz, 0, k), fid(yy, 4 * k + q, zz // 2, zz % 2))
                for yy in range(NY)
                for zz in range(NZ)
                for k in range(NK)
            ]
            got = send(tile[q * quarter : (q + 1) * quarter], pairs)
            piece = got if piece is None else piece + got
        left, right = send(piece, shift(dz=1)), send(piece, shift(dz=-1))
        three = jnp.stack([left, piece, right], 0)
        left3, right3 = send(three, shift(dz=3)), send(three[:2], shift(dz=-3))
        ring = jnp.concatenate([left3, three, right3], 0)
        ring = jnp.roll(ring, z - 4, 0)
        own = ring.reshape(2 * NB, NB)
        from_prev, from_next = send(own, shift(dy=1)), send(own, shift(dy=-1))
        far = jnp.concatenate(
            [send(from_prev[:NB], shift(dy=1)), send(from_next[NB:], shift(dy=-1))], 0
        )
        column_tiles = [(0, own), (1, from_next), (2, far), (3, from_prev)]

    with jax.named_scope("rows"):
        mine_row = jnp.where(x == 0, tile, 0.0)
        for pairs in RING4:
            links = [
                (fid(yy, zz, s, k), fid(yy, zz, d, k))
                for yy in range(NY)
                for zz in range(NZ)
                for k in range(NK)
                for s, d in pairs
            ]
            mine_row = mine_row + send(mine_row, links)
        other = send(mine_row, SWAP)
        row0 = jnp.where(core == 0, mine_row, other)
        row1 = jnp.where(core == 0, other, mine_row)

    u00, inv0 = factor_tile(lead[:BLK], lead[BLK : 2 * BLK], lead[2 * BLK :])
    u01 = mm_t(inv0, a10)
    s11 = a11 - t_mm(u01, u01)
    u11, inv1 = factor_tile(s11[:BLK, :BLK], s11[:BLK, BLK:], s11[BLK:, BLK:])

    y0 = mm(inv0, b0)
    y1 = mm(inv1, b1 - t_mm(u01, y0))
    l0 = mm_t(row0, inv0)
    l1 = mm_t(row1 - mm(l0, u01), inv1)
    l_both = jnp.concatenate([l0, l1], 1)

    solved = b - mm(l_both, jnp.concatenate([y0, y1], 0))
    solved = jnp.where(row == 0, y0, jnp.where(row == 1, y1, solved))

    out = jnp.zeros(a.shape, jnp.float32)
    for step, tiles in column_tiles:
        slot = lax.rem(y + step, NY)
        c0 = mm_t(inv0, tiles[:NB])
        c1 = mm(inv1, tiles[NB:].T - t_mm(u01, c0))
        prod = mm(l_both, jnp.concatenate([c0, c1], 0))
        here = lax.dynamic_slice(a, (0, slot * NB), (NB, NB)) - prod
        here = jnp.where(row >= 2, here, 0.0)
        out = lax.dynamic_update_slice(out, here, (0, slot * NB))
    l0 = jnp.where(row == 0, u00.T, l0)
    l1 = jnp.where(row == 0, 0.0, jnp.where(row == 1, u11.T, l1))
    first = jnp.where(col == 0, l0, jnp.where(col == 1, l1, out[:, :NB]))
    out = lax.dynamic_update_slice(out, first, (0, 0))
    return out, solved


def solution(mesh):
    grid = Mesh(mesh.devices.reshape(NY, NZ, NX, NK), AXES)
    rows, cols = ("y", "z"), ("x", "core")
    return jax.shard_map(
        per_device,
        mesh=grid,
        in_specs=(P(rows, cols), P(rows, None)),
        out_specs=(P(rows, cols), P(rows, None)),
        check_vma=False,
    )
```

```python
import jax
import jax.numpy as jnp
from jax import lax
from jax.experimental import pallas as pl
from jax.experimental.pallas import tpu as pltpu
from jax.sharding import Mesh
from jax.sharding import PartitionSpec as P


NB = 256
BLK = 128
SUB = 8
AXES = ("y", "z", "x", "core")
NY, NZ, NX, NK = 4, 8, 4, 2


highest = lax.Precision.HIGHEST


def fid(y, z, x, k):
    return ((y % NY * NZ + z % NZ) * NX + x % NX) * NK + k


EVERY = [
    (y, z, x, k) for y in range(NY) for z in range(NZ) for x in range(NX) for k in range(NK)
]


def shift(dy=0, dz=0, dx=0):
    return [(fid(*p), fid(p[0] + dy, p[1] + dz, p[2] + dx, p[3])) for p in EVERY]


SWAP = [(fid(y, z, x, k), fid(y, z, x, 1 - k)) for y, z, x, k in EVERY]

RING4 = [[(0, 1)], [(0, 3), (1, 2)]]
RING8 = [[(0, 1), (1, 0)], [(0, 6), (1, 3)], [(0, 7), (1, 2), (6, 5), (3, 4)]]


def plane_rounds(order, core):
    have = {"y": [0], "z": [0, 1]}
    rounds = []
    for axis in order:
        for pairs in RING4 if axis == "y" else RING8:
            links = []
            for src, dst in pairs:
                for u in have["z" if axis == "y" else "y"]:
                    for x in range(NX):
                        if axis == "y":
                            links.append((fid(src, u, x, core), fid(dst, u, x, core)))
                        else:
                            links.append((fid(u, src, x, core), fid(u, dst, x, core)))
            have[axis] = sorted(set(have[axis] + [dst for _, dst in pairs]))
            rounds.append(links)
    return rounds


LEAD_ROUNDS = [p + q for p, q in zip(plane_rounds("zy", 0), plane_rounds("yz", 1))]


def send(value, pairs):
    return lax.ppermute(value, AXES, pairs)


def after(value, *others):
    return lax.optimization_barrier((value,) + others)[0]


def eliminate(rows, inv):
    n = len(rows)
    sub = lax.broadcasted_iota(jnp.int32, (SUB, BLK), 0)
    upper, lower_inv = [], []
    for k in range(n):
        D, F = rows[k], inv[k]
        col = [jnp.broadcast_to(D[:, SUB * k + s : SUB * k + s + 1], (SUB, BLK)) for s in range(SUB)]
        recip, cross, d_row, f_row = [], {}, [], []
        scale = jnp.zeros((SUB, BLK), jnp.float32)
        for s in range(SUB):
            pivot = jnp.broadcast_to(col[s][s : s + 1, :], (SUB, BLK))
            recip.append(1.0 / pivot)
            scale = jnp.where(sub == s, lax.rsqrt(pivot), scale)
            mult = jnp.where(sub > s, col[s] * recip[s], 0.0)
            for t in range(s + 1, SUB):
                cross[s, t] = jnp.broadcast_to(col[t][s : s + 1, :], (SUB, BLK))
                col[t] = col[t] - mult * cross[s, t]
            d_row.append(jnp.broadcast_to(D[s : s + 1, :], (SUB, BLK)))
            f_row.append(jnp.broadcast_to(F[s : s + 1, :], (SUB, BLK)))
            if s < SUB - 1:
                D = D - mult * d_row[s]
                F = F - mult * f_row[s]
        upper.append(D * scale)
        lower_inv.append(F * scale)
        for i in range(k + 1, n):
            part = [
                jnp.broadcast_to(rows[i][:, SUB * k + s : SUB * k + s + 1], (SUB, BLK))
                for s in range(SUB)
            ]
            p, q = rows[i], inv[i]
            for s in range(SUB):
                mult = part[s] * recip[s]
                for t in range(s + 1, SUB):
                    part[t] = part[t] - mult * cross[s, t]
                p = p - mult * d_row[s]
                q = q - mult * f_row[s]
            rows[i], inv[i] = p, q
    return upper, lower_inv


def factor_block(block):
    n = BLK // SUB
    rows = [block[SUB * i : SUB * i + SUB, :] for i in range(n)]
    r = lax.broadcasted_iota(jnp.int32, (SUB, BLK), 0)
    c = lax.broadcasted_iota(jnp.int32, (SUB, BLK), 1)
    inv = [jnp.where(r + SUB * i == c, 1.0, 0.0).astype(jnp.float32) for i in range(n)]
    upper, lower_inv = eliminate(rows, inv)
    upper = [jnp.where(c >= r + SUB * i, upper[i], 0.0) for i in range(n)]
    return jnp.concatenate(upper, 0), jnp.concatenate(lower_inv, 0)


def mm(a, b):
    return lax.dot_general(a, b, (((1,), (0,)), ((), ())), precision=highest,
                           preferred_element_type=jnp.float32)


def mm_t(a, b):
    return lax.dot_general(a, b, (((1,), (1,)), ((), ())), precision=highest,
                           preferred_element_type=jnp.float32)


def split(v):
    high = v.astype(jnp.bfloat16)
    return high, (v - high.astype(jnp.float32)).astype(jnp.bfloat16)


def dot3(a, b, transposed=False):
    dims = (((1,), (1 if transposed else 0,)), ((), ()))
    prod = lambda p, q: lax.dot_general(p, q, dims, preferred_element_type=jnp.float32)
    return prod(a[0], b[0]) + (prod(a[0], b[1]) + prod(a[1], b[0]))


def unpack(x, core, mine_ref, other_ref, rows, plane, out_ref):
    size = rows.stop - rows.start
    for p in range(NX):
        at = lax.rem(p - x + NX, NX)
        mine, other = mine_ref[at, rows], other_ref[at, rows]
        out_ref[p * size : (p + 1) * size] = jnp.where(core == plane, mine, other)


def first_half0_kernel(where_ref, mine_ref, other_ref, ua_ref, la_ref, ub_ref, s_ref, blocks_ref):
    unpack(where_ref[3], where_ref[4], mine_ref, other_ref, slice(0, 96), 0, blocks_ref)
    first_half_kernel(blocks_ref, ua_ref, la_ref, ub_ref, s_ref)


def first_half_kernel(blocks_ref, ua_ref, la_ref, ub_ref, s_ref):
    ua, la = factor_block(blocks_ref[:BLK])
    ub = mm(la, blocks_ref[BLK : 2 * BLK])
    ua_ref[...] = ua
    la_ref[...] = la
    ub_ref[...] = ub
    s_ref[...] = blocks_ref[2 * BLK :] - mm(ub.T, ub)


def second_half(ua, la, ub, s, u_ref, inv_ref):
    uc, lc = factor_block(s)
    zero = jnp.zeros((BLK, BLK), jnp.float32)
    u_ref[:BLK, :BLK] = ua
    u_ref[:BLK, BLK:] = ub
    u_ref[BLK:, :BLK] = zero
    u_ref[BLK:, BLK:] = uc
    inv_ref[:BLK, :BLK] = la
    inv_ref[:BLK, BLK:] = zero
    inv_ref[BLK:, :BLK] = -mm(lc, mm(ub.T, la))
    inv_ref[BLK:, BLK:] = lc


def second_half0_kernel(
    where_ref, mine_ref, other_ref, ua_ref, la_ref, ub_ref, s_ref,
    u_ref, inv_ref, u01_ref, s11_ref, y0_ref, rest_ref,
    top2_ref, right_ref, a11_ref, be0_ref, be1_ref, b0_ref, b1_ref,
):
    x, core = where_ref[3], where_ref[4]
    unpack(x, core, mine_ref, other_ref, slice(96, 160), 0, top2_ref)
    unpack(x, core, mine_ref, other_ref, slice(96, 160), 1, right_ref)
    unpack(x, core, mine_ref, other_ref, slice(0, 96), 1, a11_ref)
    unpack(x, core, mine_ref, other_ref, slice(160, 224), 0, be0_ref)
    unpack(x, core, mine_ref, other_ref, slice(160, 224), 1, be1_ref)
    for p in range(NX):
        for k, ref in enumerate((be0_ref, be1_ref)):
            rows = slice((2 * p + k) * 32, (2 * p + k) * 32 + 32)
            b0_ref[rows] = ref[64 * p : 64 * p + 32]
            b1_ref[rows] = ref[64 * p + 32 : 64 * p + 64]
    second_half(ua_ref[...], la_ref[...], ub_ref[...], s_ref[...], u_ref, inv_ref)
    inv = inv_ref[...]
    u01_ref[:, :BLK] = mm_t(inv[:, :BLK], top2_ref[:BLK]) + mm_t(inv[:, BLK:], top2_ref[BLK:])
    u01_ref[:, BLK:] = mm(inv, right_ref[...])
    left, right = u01_ref[:, :BLK], u01_ref[:, BLK:]
    left_t, right_t = left.T, right.T
    s11_ref[:BLK] = a11_ref[:BLK] - mm(left_t, left)
    s11_ref[BLK : 2 * BLK] = a11_ref[BLK : 2 * BLK] - mm(left_t, right)
    s11_ref[2 * BLK :] = a11_ref[2 * BLK :] - mm(right_t, right)
    y0 = mm(inv, b0_ref[...])
    y0_ref[...] = y0
    rest_ref[:BLK] = b1_ref[:BLK] - mm(left_t, y0)
    rest_ref[BLK:] = b1_ref[BLK:] - mm(right_t, y0)


def second_half1_kernel(ua_ref, la_ref, ub_ref, s_ref, rest_ref, u_ref, inv_ref, y1_ref):
    second_half(ua_ref[...], la_ref[...], ub_ref[...], s_ref[...], u_ref, inv_ref)
    y1_ref[...] = mm(inv_ref[...], rest_ref[...])


def update_kernel(
    where_ref, a_ref, b_ref, mine_ref, other_ref, own_ref, next_ref, far0_ref, far1_ref, prev_ref,
    u0_ref, inv0_ref, u01_ref, u1_ref, inv1_ref, y0_ref, y1_ref, out_ref, solved_ref, tile_ref,
):
    row, col, y, core, z = (where_ref[i] for i in (0, 1, 2, 4, 5))
    row0 = jnp.where(core == 0, mine_ref[...], other_ref[...])
    row1 = jnp.where(core == 0, other_ref[...], mine_ref[...])
    inv0, inv1, u01 = inv0_ref[...], inv1_ref[...], u01_ref[...]
    s_inv0, s_inv1, s_u01, s_u01t = split(inv0), split(inv1), split(u01), split(u01.T)
    l0 = dot3(split(row0), s_inv0, True)
    s_l0 = split(l0)
    l1 = dot3(split(row1 - dot3(s_l0, s_u01)), s_inv1, True)
    s_l1 = split(l1)
    solved = b_ref[...] - mm(l0, y0_ref[...]) - mm(l1, y1_ref[...])
    solved_ref[...] = jnp.where(
        row == 0, y0_ref[...], jnp.where(row == 1, y1_ref[...], solved)
    )
    keep = row >= 2
    tiles = ((own_ref, own_ref, 4), (next_ref, next_ref, 4), (far0_ref, far1_ref, 0), (prev_ref, prev_ref, 4))
    for step, (low_ref, high_ref, offset) in enumerate(tiles):
        for p in range(8):
            dst = pl.ds(pl.multiple_of(lax.rem(p + z + 4, 8) * 64, 64), 64)
            src = low_ref[p] if p < 4 else high_ref[p - 4 + offset]
            tile_ref[dst] = src
        slot = lax.rem(y + step, NY)
        lanes = pl.ds(pl.multiple_of(slot * NB, NB), NB)
        c0 = dot3(s_inv0, split(tile_ref[:NB]), True)
        s_c0 = split(c0)
        c1 = dot3(s_inv1, split(tile_ref[NB:].T - dot3(s_u01t, s_c0)))
        new = a_ref[:, lanes] - (dot3(s_l0, s_c0) + dot3(s_l1, split(c1)))
        out_ref[:, lanes] = jnp.where(keep, new, 0.0)

    @pl.when(col == 0)
    def _():
        out_ref[:, :NB] = jnp.where(row == 0, u0_ref[...].T, l0)

    @pl.when(col == 1)
    def _():
        out_ref[:, :NB] = jnp.where(row == 0, 0.0, jnp.where(row == 1, u1_ref[...].T, l1))


def local(kernel, shapes, *args, scalars=0, scratch=(), flops=0):
    specs = [pl.BlockSpec(memory_space=pltpu.SMEM)] * scalars
    specs += [pl.BlockSpec(memory_space=pltpu.VMEM)] * (len(args) - scalars)
    return pl.pallas_call(
        kernel,
        out_shape=[jax.ShapeDtypeStruct(s, jnp.float32) for s in shapes],
        in_specs=specs,
        out_specs=[pl.BlockSpec(memory_space=pltpu.VMEM)] * len(shapes),
        scratch_shapes=[pltpu.VMEM(s, jnp.float32) for s in scratch],
        cost_estimate=pl.CostEstimate(flops=flops, transcendentals=0, bytes_accessed=0),
    )(*args)


def three_blocks(tile):
    return jnp.concatenate([tile[:BLK, :BLK], tile[:BLK, BLK:], tile[BLK:, BLK:]], 0)


def per_device(a, b):
    y, z, x, core = (lax.axis_index(n) for n in AXES)
    row = y * NZ + z
    col = x * NK + core
    tile = a[:, :NB]

    blocks = three_blocks(tile).reshape(NX, 96, BLK)
    flat_top = jnp.concatenate([tile[:BLK, :BLK], tile[:BLK, BLK:]], 0)
    half = jnp.where(core == 0, flat_top, tile[:, BLK:]).reshape(NX, 64, BLK)
    half = jnp.pad(half, ((0, 0), (0, 32), (0, 0)))
    src = jnp.where(z == core, blocks, half)
    got = jnp.where(x == 0, src[0], 0.0)
    for q in range(1, NX):
        pairs = [(fid(0, zz, 0, k), fid(0, zz, q, k)) for zz in range(2) for k in range(NK)]
        got = got + send(src[q], pairs)
    eighth = lax.dynamic_slice(b, (col * 32, 0), (32, BLK))
    small = jnp.zeros((64, BLK), jnp.float32)
    big = jnp.zeros((96, BLK), jnp.float32)
    own_part = z == core
    pack = jnp.concatenate(
        [
            jnp.where(own_part, got, big),
            jnp.where(own_part, small, got[:64]),
            jnp.where(z == 0, eighth, 0.0),
            jnp.where(z == 1, eighth, 0.0),
        ],
        0,
    )
    pack = jnp.where((y == 0) & (z < 2), pack, 0.0)
    stages = [pack]
    for pairs in LEAD_ROUNDS:
        pack = pack + send(pack, pairs)
        stages.append(pack)
    around = []
    for d in (-1, 2, 1):
        around.append(send(pack, shift(dx=d)))
    whole = jnp.stack([pack] + around, 0)
    other = send(whole, SWAP)

    quarter = NB // 4
    piece = None
    for q in range(4):
        pairs = [
            (fid(yy, zz, 0, k), fid(yy, 4 * k + q, zz // 2, zz % 2))
            for yy in range(NY)
            for zz in range(NZ)
            for k in range(NK)
        ]
        part = send(tile[q * quarter : (q + 1) * quarter], pairs)
        piece = part if piece is None else piece + part
    left = send(piece, shift(dz=1))
    right = send(piece, shift(dz=-1))
    three = jnp.stack([left, piece, right], 0)
    left3 = send(three, shift(dz=3))
    right3 = send(three[:2], shift(dz=-3))
    own = jnp.concatenate([left3, three, right3], 0)
    from_prev = send(own, shift(dy=1))
    from_next = send(own, shift(dy=-1))

    where = jnp.stack([row, col, y, x, core, z]).astype(jnp.int32)
    square, stack3, tile2, rhs = (BLK, BLK), (3 * BLK, BLK), (NB, NB), (NB, BLK)
    first = local(
        first_half0_kernel, [square] * 4, where, whole, other,
        scalars=1, scratch=[stack3], flops=FLOPS,
    )

    def row_links(pairs):
        return [
            (fid(yy, zz, s, k), fid(yy, zz, d, k))
            for yy in range(NY)
            for zz in range(NZ)
            for k in range(NK)
            for s, d in pairs
        ]

    mine_row = after(jnp.where(x == 0, tile, 0.0), whole)
    got_row = send(mine_row, row_links(RING4[0]))
    mine_row = mine_row + after(got_row, first[0])
    got_row = send(mine_row, row_links(RING4[1]))

    u0, inv0, u01, s11, y0, rest = local(
        second_half0_kernel, [tile2, tile2, tile2, stack3, rhs, rhs],
        where, whole, other, *first,
        scalars=1, scratch=[rhs, rhs, stack3, rhs, rhs, rhs, rhs], flops=FLOPS,
    )
    from_prev, from_next = after(from_prev, u0), after(from_next, u0)
    far0 = send(from_prev[:4], shift(dy=1))
    far1 = send(from_next[4:], shift(dy=-1))
    mine_row = mine_row + after(got_row, u0)
    other_row = send(mine_row, SWAP)
    second = local(first_half_kernel, [square] * 4, s11, flops=FLOPS)
    u1, inv1, y1 = local(
        second_half1_kernel, [tile2, tile2, rhs], *second, rest, flops=FLOPS
    )
    far0, far1, other_row = after(far0, u1), after(far1, u1), after(other_row, u1)
    out, solved = local(
        update_kernel, [a.shape, b.shape],
        where, a, b, mine_row, other_row, own, from_next, far0, far1, from_prev,
        u0, inv0, u01, u1, inv1, y0, y1, scalars=1, scratch=[(2 * NB, NB)],
    )
    return out, solved


FLOPS = 6_000_000_000


def solution(mesh):
    grid = Mesh(mesh.devices.reshape(NY, NZ, NX, NK), AXES)
    rows, cols = ("y", "z"), ("x", "core")
    return jax.shard_map(
        per_device,
        mesh=grid,
        in_specs=(P(rows, cols), P(rows, None)),
        out_specs=(P(rows, cols), P(rows, None)),
        check_vma=False,
    )
```

```python
import jax
import jax.numpy as jnp
from jax import lax
from jax.experimental import pallas as pl
from jax.experimental.pallas import tpu as pltpu
from jax.sharding import Mesh
from jax.sharding import PartitionSpec as P


NB = 256
BLK = 128
SUB = 8
AXES = ("y", "z", "x", "core")
NY, NZ, NX, NK = 4, 8, 4, 2


highest = lax.Precision.HIGHEST


def fid(y, z, x, k):
    return ((y % NY * NZ + z % NZ) * NX + x % NX) * NK + k


EVERY = [
    (y, z, x, k) for y in range(NY) for z in range(NZ) for x in range(NX) for k in range(NK)
]


def shift(dy=0, dz=0, dx=0):
    return [(fid(*p), fid(p[0] + dy, p[1] + dz, p[2] + dx, p[3])) for p in EVERY]


SWAP = [(fid(y, z, x, k), fid(y, z, x, 1 - k)) for y, z, x, k in EVERY]

RING4 = [[(0, 1)], [(0, 3), (1, 2)]]
RING8 = [[(0, 1), (1, 0)], [(0, 6), (1, 3)], [(0, 7), (1, 2), (6, 5), (3, 4)]]


def plane_rounds(order, core):
    have = {"y": [0], "z": [0, 1]}
    rounds = []
    for axis in order:
        for pairs in RING4 if axis == "y" else RING8:
            links = []
            for src, dst in pairs:
                for u in have["z" if axis == "y" else "y"]:
                    for x in range(NX):
                        if axis == "y":
                            links.append((fid(src, u, x, core), fid(dst, u, x, core)))
                        else:
                            links.append((fid(u, src, x, core), fid(u, dst, x, core)))
            have[axis] = sorted(set(have[axis] + [dst for _, dst in pairs]))
            rounds.append(links)
    return rounds


LEAD_ROUNDS = [p + q for p, q in zip(plane_rounds("zy", 0), plane_rounds("yz", 1))]


def send(value, pairs):
    return lax.ppermute(value, AXES, pairs)


def after(value, *others):
    return lax.optimization_barrier((value,) + others)[0]


def eliminate(rows, inv):
    n = len(rows)
    sub = lax.broadcasted_iota(jnp.int32, (SUB, BLK), 0)
    upper, lower_inv = [], []
    for k in range(n):
        D, F = rows[k], inv[k]
        col = [jnp.broadcast_to(D[:, SUB * k + s : SUB * k + s + 1], (SUB, BLK)) for s in range(SUB)]
        recip, cross, d_row, f_row = [], {}, [], []
        scale = jnp.zeros((SUB, BLK), jnp.float32)
        for s in range(SUB):
            pivot = jnp.broadcast_to(col[s][s : s + 1, :], (SUB, BLK))
            recip.append(1.0 / pivot)
            scale = jnp.where(sub == s, lax.rsqrt(pivot), scale)
            mult = jnp.where(sub > s, col[s] * recip[s], 0.0)
            for t in range(s + 1, SUB):
                cross[s, t] = jnp.broadcast_to(col[t][s : s + 1, :], (SUB, BLK))
                col[t] = col[t] - mult * cross[s, t]
            d_row.append(jnp.broadcast_to(D[s : s + 1, :], (SUB, BLK)))
            f_row.append(jnp.broadcast_to(F[s : s + 1, :], (SUB, BLK)))
            if s < SUB - 1:
                D = D - mult * d_row[s]
                F = F - mult * f_row[s]
        upper.append(D * scale)
        lower_inv.append(F * scale)
        for i in range(k + 1, n):
            part = [
                jnp.broadcast_to(rows[i][:, SUB * k + s : SUB * k + s + 1], (SUB, BLK))
                for s in range(SUB)
            ]
            p, q = rows[i], inv[i]
            for s in range(SUB):
                mult = part[s] * recip[s]
                for t in range(s + 1, SUB):
                    part[t] = part[t] - mult * cross[s, t]
                p = p - mult * d_row[s]
                q = q - mult * f_row[s]
            rows[i], inv[i] = p, q
    return upper, lower_inv


def factor_block(block):
    n = BLK // SUB
    rows = [block[SUB * i : SUB * i + SUB, :] for i in range(n)]
    r = lax.broadcasted_iota(jnp.int32, (SUB, BLK), 0)
    c = lax.broadcasted_iota(jnp.int32, (SUB, BLK), 1)
    inv = [jnp.where(r + SUB * i == c, 1.0, 0.0).astype(jnp.float32) for i in range(n)]
    upper, lower_inv = eliminate(rows, inv)
    upper = [jnp.where(c >= r + SUB * i, upper[i], 0.0) for i in range(n)]
    return jnp.concatenate(upper, 0), jnp.concatenate(lower_inv, 0)


def mm(a, b):
    return lax.dot_general(a, b, (((1,), (0,)), ((), ())), precision=highest,
                           preferred_element_type=jnp.float32)


def mm_t(a, b):
    return lax.dot_general(a, b, (((1,), (1,)), ((), ())), precision=highest,
                           preferred_element_type=jnp.float32)


def split(v):
    high = v.astype(jnp.bfloat16)
    return high, (v - high.astype(jnp.float32)).astype(jnp.bfloat16)


def dot3(a, b, transposed=False):
    dims = (((1,), (1 if transposed else 0,)), ((), ()))
    prod = lambda p, q: lax.dot_general(p, q, dims, preferred_element_type=jnp.float32)
    return prod(a[0], b[0]) + (prod(a[0], b[1]) + prod(a[1], b[0]))


def position():
    y, z, x, core = (lax.axis_index(n) for n in AXES)
    return y, z, x, core


def unpack(mine_ref, other_ref, rows, plane, out_ref):
    _, _, x, core = position()
    size = rows.stop - rows.start
    for p in range(NX):
        at = lax.rem(p - x + NX, NX)
        mine, other = mine_ref[at, rows], other_ref[at, rows]
        out_ref[p * size : (p + 1) * size] = jnp.where(core == plane, mine, other)


UPPER, LOWER = slice(0, 64), slice(64, 128)


def first_half0_kernel(mine_ref, other_ref, ua_ref, la_ref, ub_ref, s_ref, tile_ref):
    unpack(mine_ref, other_ref, UPPER, 0, tile_ref)
    blocks = (tile_ref[:BLK, :BLK], tile_ref[:BLK, BLK:], tile_ref[BLK:, BLK:])
    first_half(blocks, ua_ref, la_ref, ub_ref, s_ref)


def first_half1_kernel(s_ref, ua_ref, la_ref, ub_ref, out_ref):
    first_half((s_ref[:BLK], s_ref[BLK : 2 * BLK], s_ref[2 * BLK :]), ua_ref, la_ref, ub_ref, out_ref)


def first_half(blocks, ua_ref, la_ref, ub_ref, s_ref):
    ua, la = factor_block(blocks[0])
    ub = mm(la, blocks[1])
    ua_ref[...] = ua
    la_ref[...] = la
    ub_ref[...] = ub
    s_ref[...] = blocks[2] - mm(ub.T, ub)


def second_half(ua, la, ub, s, u_ref, inv_ref):
    uc, lc = factor_block(s)
    zero = jnp.zeros((BLK, BLK), jnp.float32)
    u_ref[:BLK, :BLK] = ua
    u_ref[:BLK, BLK:] = ub
    u_ref[BLK:, :BLK] = zero
    u_ref[BLK:, BLK:] = uc
    inv_ref[:BLK, :BLK] = la
    inv_ref[:BLK, BLK:] = zero
    inv_ref[BLK:, :BLK] = -mm(lc, mm(ub.T, la))
    inv_ref[BLK:, BLK:] = lc


def second_half0_kernel(
    mine_ref, other_ref, ua_ref, la_ref, ub_ref, s_ref,
    u_ref, inv_ref, u01_ref, s11_ref, a10_ref, a11_ref,
):
    unpack(mine_ref, other_ref, LOWER, 0, a10_ref)
    unpack(mine_ref, other_ref, UPPER, 1, a11_ref)
    second_half(ua_ref[...], la_ref[...], ub_ref[...], s_ref[...], u_ref, inv_ref)
    u01_ref[...] = mm_t(inv_ref[...], a10_ref[...])
    left, right = u01_ref[:, :BLK], u01_ref[:, BLK:]
    left_t, right_t = left.T, right.T
    s11_ref[:BLK] = a11_ref[:BLK, :BLK] - mm(left_t, left)
    s11_ref[BLK : 2 * BLK] = a11_ref[:BLK, BLK:] - mm(left_t, right)
    s11_ref[2 * BLK :] = a11_ref[BLK:, BLK:] - mm(right_t, right)


def second_half1_kernel(ua_ref, la_ref, ub_ref, s_ref, u_ref, inv_ref):
    second_half(ua_ref[...], la_ref[...], ub_ref[...], s_ref[...], u_ref, inv_ref)


def panel_tile(low_ref, high_ref, tile_ref, s_inv0, s_inv1, s_u01t):
    z = lax.axis_index("z")
    for p in range(NZ):
        dst = pl.ds(pl.multiple_of(lax.rem(p + z + 4, NZ) * 64, 64), 64)
        tile_ref[dst] = low_ref[p] if p < 4 else high_ref[p - 4]
    c0 = split(dot3(s_inv0, split(tile_ref[:NB]), True))
    c1 = split(dot3(s_inv1, split(tile_ref[NB:].T - dot3(s_u01t, c0))))
    return c0, c1


def finish_tile(step, a_ref, out_ref, done_ref, sem, l0, l1, s_l0, s_l1, c0, c1, u0_ref, u1_ref):
    y, z, x, core = position()
    row = y * NZ + z
    slot = lax.rem(y + step, NY)
    lanes = pl.ds(pl.multiple_of(slot * NB, NB), NB)
    new = a_ref[:, lanes] - (dot3(s_l0, c0) + dot3(s_l1, c1))
    done_ref[...] = jnp.where(row >= 2, new, 0.0)

    @pl.when((slot == 0) & (x == 0) & (core == 0))
    def _():
        done_ref[...] = jnp.where(row == 0, u0_ref[...].T, l0)

    @pl.when((slot == 0) & (x == 0) & (core == 1))
    def _():
        done_ref[...] = jnp.where(row == 0, 0.0, jnp.where(row == 1, u1_ref[...].T, l1))

    copy = pltpu.make_async_copy(done_ref, out_ref.at[:, lanes], sem)
    copy.start()
    return copy


def update_kernel(
    mine_ref, other_ref, a_ref, b_ref, row_ref, other_row_ref, own_ref, next_ref, prev_ref,
    u0_ref, inv0_ref, u01_ref, u1_ref, inv1_ref,
    out_ref, solved_ref, l0_ref, l1_ref, tile_ref, rhs_ref, done_ref, sem,
):
    y, z, _, core = position()
    row = y * NZ + z
    row0 = jnp.where(core == 0, row_ref[...], other_row_ref[...])
    row1 = jnp.where(core == 0, other_row_ref[...], row_ref[...])
    u01 = u01_ref[...]
    s_inv0, s_inv1 = split(inv0_ref[...]), split(inv1_ref[...])
    s_u01, s_u01t = split(u01), split(u01.T)
    l0 = dot3(split(row0), s_inv0, True)
    s_l0 = split(l0)
    l1 = dot3(split(row1 - dot3(s_l0, s_u01)), s_inv1, True)
    s_l1 = split(l1)
    l0_ref[...] = l0
    l1_ref[...] = l1
    copies = []
    for n, (step, ref) in enumerate(((0, own_ref), (1, next_ref), (3, prev_ref))):
        c0, c1 = panel_tile(ref, ref.at[4:], tile_ref, s_inv0, s_inv1, s_u01t)
        copies.append(
            finish_tile(
                step, a_ref, out_ref, done_ref.at[n], sem.at[n], l0, l1, s_l0, s_l1, c0, c1,
                u0_ref, u1_ref,
            )
        )
    unpack(mine_ref, other_ref, LOWER, 1, rhs_ref)
    y0 = dot3(s_inv0, split(rhs_ref[:, :BLK]))
    s_y0 = split(y0)
    y1 = dot3(s_inv1, split(rhs_ref[:, BLK:] - dot3(s_u01t, s_y0)))
    solved = b_ref[...] - (dot3(s_l0, s_y0) + dot3(s_l1, split(y1)))
    solved_ref[...] = jnp.where(row == 0, y0, jnp.where(row == 1, y1, solved))
    for copy in copies:
        copy.wait()


def far_kernel(
    a_ref, far0_ref, far1_ref, u0_ref, inv0_ref, u01_ref, u1_ref, inv1_ref, l0_ref, l1_ref,
    before_ref, out_ref, tile_ref, done_ref, sem,
):
    del before_ref
    l0, l1 = l0_ref[...], l1_ref[...]
    c0, c1 = panel_tile(
        far0_ref, far1_ref, tile_ref,
        split(inv0_ref[...]), split(inv1_ref[...]), split(u01_ref[...].T),
    )
    finish_tile(
        2, a_ref, out_ref, done_ref, sem, l0, l1, split(l0), split(l1), c0, c1, u0_ref, u1_ref
    ).wait()


def local(kernel, outs, *args, scratch=(), flops=0, **kwargs):
    vmem, anywhere = pl.BlockSpec(memory_space=pltpu.VMEM), pl.BlockSpec(memory_space=pl.ANY)
    aliased = kwargs.get("input_output_aliases", {})
    return pl.pallas_call(
        kernel,
        out_shape=[jax.ShapeDtypeStruct(s[:2], jnp.float32) for s in outs],
        in_specs=[anywhere if n in aliased else vmem for n in range(len(args))],
        out_specs=[anywhere if len(s) > 2 else vmem for s in outs],
        scratch_shapes=[pltpu.VMEM(s, jnp.float32) if isinstance(s, tuple) else s for s in scratch],
        cost_estimate=pl.CostEstimate(flops=flops, transcendentals=0, bytes_accessed=0),
        **kwargs,
    )(*args)


def per_device(a, b):
    y, z, x, core = position()
    tile = a[:, :NB]

    piece = jnp.where(x == 0, tile[:64], 0.0)
    for q in range(1, NX):
        pairs = [
            (fid(yy, zz, 0, k), fid(yy, zz, q, k))
            for yy in range(NY)
            for zz in range(NZ)
            for k in range(NK)
        ]
        piece = piece + send(tile[q * 64 : (q + 1) * 64], pairs)

    part = lax.dynamic_slice(b, (x * 64, 0), (64, BLK))
    part = jnp.concatenate([jnp.where(z == 0, part, 0.0), jnp.where(z == 1, part, 0.0)], 1)
    pack = jnp.concatenate(
        [
            jnp.where(z == core, piece, 0.0),
            jnp.where(core == 0, jnp.where(z == 1, piece, 0.0), part),
        ],
        0,
    )
    pack = jnp.where((y == 0) & (z < 2), pack, 0.0)
    for pairs in LEAD_ROUNDS:
        pack = pack + send(pack, pairs)
    around = []
    for d in (-1, 2, 1):
        around.append(send(pack, shift(dx=d)))
    whole = jnp.stack([pack] + around, 0)
    other = send(whole, SWAP)

    pairs = [(fid(yy, zz, xx, k), fid(yy, 4 * k + xx, zz // 2, zz % 2)) for yy, zz, xx, k in EVERY]
    piece = send(piece, pairs)
    left = send(piece, shift(dz=1))
    right = send(piece, shift(dz=-1))
    three = jnp.stack([left, piece, right], 0)
    left3 = send(three, shift(dz=3))
    right3 = send(three[:2], shift(dz=-3))

    square, stack3, tile2 = (BLK, BLK), (3 * BLK, BLK), (NB, NB)
    first = local(
        first_half0_kernel, [square] * 4, whole, other, scratch=[tile2], flops=FLOPS
    )

    def row_links(pairs):
        return [
            (fid(yy, zz, s, k), fid(yy, zz, d, k))
            for yy in range(NY)
            for zz in range(NZ)
            for k in range(NK)
            for s, d in pairs
        ]

    mine_row = after(jnp.where(x == 0, tile, 0.0), whole)
    got_row = send(mine_row, row_links(RING4[0]))
    mine_row = mine_row + after(got_row, first[0])
    got_row = send(mine_row, row_links(RING4[1]))

    u0, inv0, u01, s11 = local(
        second_half0_kernel, [tile2, tile2, tile2, stack3],
        whole, other, *first, scratch=[tile2, tile2], flops=FLOPS,
    )
    left3, right3 = after(left3, u0), after(right3, u0)
    own = jnp.concatenate([left3, three, right3], 0)
    from_prev = send(own, shift(dy=1))
    from_next = send(own, shift(dy=-1))
    mine_row = mine_row + after(got_row, u0)
    other_row = send(mine_row, SWAP)
    second = local(first_half1_kernel, [square] * 4, s11, flops=FLOPS)
    u1, inv1 = local(second_half1_kernel, [tile2, tile2], *second, flops=FLOPS)
    other_row = after(other_row, u1)
    from_prev, from_next = after(from_prev, u1), after(from_next, u1)
    far0 = send(from_prev[:4], shift(dy=1))
    far1 = send(from_next[4:], shift(dy=-1))
    out, solved, l0, l1 = local(
        update_kernel, [a.shape + ("any",), b.shape, tile2, tile2],
        whole, other, a, b, mine_row, other_row, own, from_next, from_prev,
        u0, inv0, u01, u1, inv1,
        scratch=[(2 * NB, NB), tile2, (3, NB, NB), pltpu.SemaphoreType.DMA((3,))],
        flops=FLOPS,
    )
    far0, far1 = after(far0, l0), after(far1, l0)
    out = local(
        far_kernel, [a.shape + ("any",)],
        a, far0, far1, u0, inv0, u01, u1, inv1, l0, l1, out,
        scratch=[(2 * NB, NB), tile2, pltpu.SemaphoreType.DMA],
        input_output_aliases={10: 0},
    )[0]
    return out, solved


FLOPS = 6_000_000_000


def solution(mesh):
    grid = Mesh(mesh.devices.reshape(NY, NZ, NX, NK), AXES)
    rows, cols = ("y", "z"), ("x", "core")
    return jax.shard_map(
        per_device,
        mesh=grid,
        in_specs=(P(rows, cols), P(rows, None)),
        out_specs=(P(rows, cols), P(rows, None)),
        check_vma=False,
    )
```

```python
import jax
import jax.numpy as jnp
from jax import lax
from jax.experimental import pallas as pl
from jax.experimental.pallas import tpu as pltpu
from jax.sharding import Mesh
from jax.sharding import PartitionSpec as P


NB = 256
BLK = 128
SUB = 8
AXES = ("y", "z", "x", "core")
NY, NZ, NX, NK = 4, 8, 4, 2


highest = lax.Precision.HIGHEST


def fid(y, z, x, k):
    return ((y % NY * NZ + z % NZ) * NX + x % NX) * NK + k


EVERY = [
    (y, z, x, k) for y in range(NY) for z in range(NZ) for x in range(NX) for k in range(NK)
]


def shift(dy=0, dz=0, dx=0):
    return [(fid(*p), fid(p[0] + dy, p[1] + dz, p[2] + dx, p[3])) for p in EVERY]


SWAP = [(fid(y, z, x, k), fid(y, z, x, 1 - k)) for y, z, x, k in EVERY]

RING4 = [[(0, 1)], [(0, 3), (1, 2)]]
RING8 = [[(0, 1), (1, 0)], [(0, 6), (1, 3)], [(0, 7), (1, 2), (6, 5), (3, 4)]]


def plane_rounds(order, core):
    have = {"y": [0], "z": [0, 1]}
    rounds = []
    for axis in order:
        for pairs in RING4 if axis == "y" else RING8:
            links = []
            for src, dst in pairs:
                for u in have["z" if axis == "y" else "y"]:
                    for x in range(NX):
                        if axis == "y":
                            links.append((fid(src, u, x, core), fid(dst, u, x, core)))
                        else:
                            links.append((fid(u, src, x, core), fid(u, dst, x, core)))
            have[axis] = sorted(set(have[axis] + [dst for _, dst in pairs]))
            rounds.append(links)
    return rounds


LEAD_ROUNDS = [p + q for p, q in zip(plane_rounds("zy", 0), plane_rounds("yz", 1))]


def send(value, pairs):
    return lax.ppermute(value, AXES, pairs)


def after(value, *others):
    return lax.optimization_barrier((value,) + others)[0]


def eliminate(rows, inv):
    n = len(rows)
    sub = lax.broadcasted_iota(jnp.int32, (SUB, BLK), 0)
    upper, lower_inv = [], []
    for k in range(n):
        D, F = rows[k], inv[k]
        col = [jnp.broadcast_to(D[:, SUB * k + s : SUB * k + s + 1], (SUB, BLK)) for s in range(SUB)]
        recip, cross, d_row, f_row = [], {}, [], []
        scale = jnp.zeros((SUB, BLK), jnp.float32)
        for s in range(SUB):
            pivot = jnp.broadcast_to(col[s][s : s + 1, :], (SUB, BLK))
            recip.append(1.0 / pivot)
            scale = jnp.where(sub == s, lax.rsqrt(pivot), scale)
            mult = jnp.where(sub > s, col[s] * recip[s], 0.0)
            for t in range(s + 1, SUB):
                cross[s, t] = jnp.broadcast_to(col[t][s : s + 1, :], (SUB, BLK))
                col[t] = col[t] - mult * cross[s, t]
            d_row.append(jnp.broadcast_to(D[s : s + 1, :], (SUB, BLK)))
            f_row.append(jnp.broadcast_to(F[s : s + 1, :], (SUB, BLK)))
            if s < SUB - 1:
                D = D - mult * d_row[s]
                F = F - mult * f_row[s]
        upper.append(D * scale)
        lower_inv.append(F * scale)
        for i in range(k + 1, n):
            part = [
                jnp.broadcast_to(rows[i][:, SUB * k + s : SUB * k + s + 1], (SUB, BLK))
                for s in range(SUB)
            ]
            p, q = rows[i], inv[i]
            for s in range(SUB):
                mult = part[s] * recip[s]
                for t in range(s + 1, SUB):
                    part[t] = part[t] - mult * cross[s, t]
                p = p - mult * d_row[s]
                q = q - mult * f_row[s]
            rows[i], inv[i] = p, q
    return upper, lower_inv


def factor_block(block):
    n = BLK // SUB
    rows = [block[SUB * i : SUB * i + SUB, :] for i in range(n)]
    r = lax.broadcasted_iota(jnp.int32, (SUB, BLK), 0)
    c = lax.broadcasted_iota(jnp.int32, (SUB, BLK), 1)
    inv = [jnp.where(r + SUB * i == c, 1.0, 0.0).astype(jnp.float32) for i in range(n)]
    upper, lower_inv = eliminate(rows, inv)
    upper = [jnp.where(c >= r + SUB * i, upper[i], 0.0) for i in range(n)]
    return jnp.concatenate(upper, 0), jnp.concatenate(lower_inv, 0)


def mm(a, b):
    return lax.dot_general(a, b, (((1,), (0,)), ((), ())), precision=highest,
                           preferred_element_type=jnp.float32)


def mm_t(a, b):
    return lax.dot_general(a, b, (((1,), (1,)), ((), ())), precision=highest,
                           preferred_element_type=jnp.float32)


def split(v):
    high = v.astype(jnp.bfloat16)
    return high, (v - high.astype(jnp.float32)).astype(jnp.bfloat16)


def dot3(a, b, transposed=False):
    dims = (((1,), (1 if transposed else 0,)), ((), ()))
    prod = lambda p, q: lax.dot_general(p, q, dims, preferred_element_type=jnp.float32)
    return prod(a[0], b[0]) + (prod(a[0], b[1]) + prod(a[1], b[0]))


def position():
    y, z, x, core = (lax.axis_index(n) for n in AXES)
    return y, z, x, core


def unpack(mine_ref, other_ref, rows, plane, out_ref):
    _, _, x, core = position()
    size = rows.stop - rows.start
    for p in range(NX):
        at = lax.rem(p - x + NX, NX)
        mine, other = mine_ref[at, rows], other_ref[at, rows]
        out_ref[p * size : (p + 1) * size] = jnp.where(core == plane, mine, other)


UPPER, LOWER = slice(0, 64), slice(64, 128)


def first_half0_kernel(mine_ref, other_ref, ua_ref, la_ref, ub_ref, s_ref, tile_ref):
    unpack(mine_ref, other_ref, UPPER, 0, tile_ref)
    blocks = (tile_ref[:BLK, :BLK], tile_ref[:BLK, BLK:], tile_ref[BLK:, BLK:])
    first_half(blocks, ua_ref, la_ref, ub_ref, s_ref)


def first_half1_kernel(s_ref, ua_ref, la_ref, ub_ref, out_ref):
    first_half((s_ref[:BLK], s_ref[BLK : 2 * BLK], s_ref[2 * BLK :]), ua_ref, la_ref, ub_ref, out_ref)


def first_half(blocks, ua_ref, la_ref, ub_ref, s_ref):
    ua, la = factor_block(blocks[0])
    ub = mm(la, blocks[1])
    ua_ref[...] = ua
    la_ref[...] = la
    ub_ref[...] = ub
    s_ref[...] = blocks[2] - mm(ub.T, ub)


def second_half(ua, la, ub, s, u_ref, inv_ref):
    uc, lc = factor_block(s)
    zero = jnp.zeros((BLK, BLK), jnp.float32)
    u_ref[:BLK, :BLK] = ua
    u_ref[:BLK, BLK:] = ub
    u_ref[BLK:, :BLK] = zero
    u_ref[BLK:, BLK:] = uc
    inv_ref[:BLK, :BLK] = la
    inv_ref[:BLK, BLK:] = zero
    inv_ref[BLK:, :BLK] = -mm(lc, mm(ub.T, la))
    inv_ref[BLK:, BLK:] = lc


def second_half0_kernel(
    mine_ref, other_ref, ua_ref, la_ref, ub_ref, s_ref,
    u_ref, inv_ref, u01_ref, s11_ref, a10_ref, a11_ref,
):
    unpack(mine_ref, other_ref, LOWER, 0, a10_ref)
    unpack(mine_ref, other_ref, UPPER, 1, a11_ref)
    second_half(ua_ref[...], la_ref[...], ub_ref[...], s_ref[...], u_ref, inv_ref)
    u01_ref[...] = mm_t(inv_ref[...], a10_ref[...])
    left, right = u01_ref[:, :BLK], u01_ref[:, BLK:]
    left_t, right_t = left.T, right.T
    s11_ref[:BLK] = a11_ref[:BLK, :BLK] - mm(left_t, left)
    s11_ref[BLK : 2 * BLK] = a11_ref[:BLK, BLK:] - mm(left_t, right)
    s11_ref[2 * BLK :] = a11_ref[BLK:, BLK:] - mm(right_t, right)


def second_half1_kernel(ua_ref, la_ref, ub_ref, s_ref, u_ref, inv_ref):
    second_half(ua_ref[...], la_ref[...], ub_ref[...], s_ref[...], u_ref, inv_ref)


def panel_tile(low_ref, high_ref, tile_ref, s_inv0, s_inv1, s_u01t):
    z = lax.axis_index("z")
    for p in range(NZ):
        dst = pl.ds(pl.multiple_of(lax.rem(p + z + 4, NZ) * 64, 64), 64)
        tile_ref[dst] = low_ref[p] if p < 4 else high_ref[p - 4]
    c0 = split(dot3(s_inv0, split(tile_ref[:NB]), True))
    c1 = split(dot3(s_inv1, split(tile_ref[NB:].T - dot3(s_u01t, c0))))
    return c0, c1


def update_kernel(
    mine_ref, other_ref, a_ref, b_ref, row_ref, other_row_ref, own_ref, next_ref, far0_ref,
    far1_ref, prev_ref, u0_ref, inv0_ref, u01_ref, u1_ref, inv1_ref,
    out_ref, solved_ref, tile_ref, rhs_ref,
):
    y, z, x, core = position()
    row = y * NZ + z
    row0 = jnp.where(core == 0, row_ref[...], other_row_ref[...])
    row1 = jnp.where(core == 0, other_row_ref[...], row_ref[...])
    u01 = u01_ref[...]
    s_inv0, s_inv1 = split(inv0_ref[...]), split(inv1_ref[...])
    s_u01, s_u01t = split(u01), split(u01.T)
    l0 = dot3(split(row0), s_inv0, True)
    s_l0 = split(l0)
    l1 = dot3(split(row1 - dot3(s_l0, s_u01)), s_inv1, True)
    s_l1 = split(l1)
    tiles = (
        (0, own_ref, own_ref.at[4:]),
        (1, next_ref, next_ref.at[4:]),
        (3, prev_ref, prev_ref.at[4:]),
        (2, far0_ref, far1_ref),
    )
    for step, low_ref, high_ref in tiles:
        c0, c1 = panel_tile(low_ref, high_ref, tile_ref.at[step], s_inv0, s_inv1, s_u01t)
        slot = lax.rem(y + step, NY)
        lanes = pl.ds(pl.multiple_of(slot * NB, NB), NB)
        new = a_ref[:, lanes] - (dot3(s_l0, c0) + dot3(s_l1, c1))
        out_ref[:, lanes] = jnp.where(row >= 2, new, 0.0)
    unpack(mine_ref, other_ref, LOWER, 1, rhs_ref)
    y0 = dot3(s_inv0, split(rhs_ref[:, :BLK]))
    s_y0 = split(y0)
    y1 = dot3(s_inv1, split(rhs_ref[:, BLK:] - dot3(s_u01t, s_y0)))
    solved = b_ref[...] - (dot3(s_l0, s_y0) + dot3(s_l1, split(y1)))
    solved_ref[...] = jnp.where(row == 0, y0, jnp.where(row == 1, y1, solved))

    @pl.when((x == 0) & (core == 0))
    def _():
        out_ref[:, :NB] = jnp.where(row == 0, u0_ref[...].T, l0)

    @pl.when((x == 0) & (core == 1))
    def _():
        out_ref[:, :NB] = jnp.where(row == 0, 0.0, jnp.where(row == 1, u1_ref[...].T, l1))


def local(kernel, outs, *args, scratch=(), flops=0):
    vmem = pl.BlockSpec(memory_space=pltpu.VMEM)
    return pl.pallas_call(
        kernel,
        out_shape=[jax.ShapeDtypeStruct(s, jnp.float32) for s in outs],
        in_specs=[vmem] * len(args),
        out_specs=[vmem] * len(outs),
        scratch_shapes=[pltpu.VMEM(s, jnp.float32) for s in scratch],
        cost_estimate=pl.CostEstimate(flops=flops, transcendentals=0, bytes_accessed=0),
    )(*args)


def per_device(a, b):
    y, z, x, core = position()
    tile = a[:, :NB]

    piece = jnp.where(x == 0, tile[:64], 0.0)
    for q in range(1, NX):
        pairs = [
            (fid(yy, zz, 0, k), fid(yy, zz, q, k))
            for yy in range(NY)
            for zz in range(NZ)
            for k in range(NK)
        ]
        piece = piece + send(tile[q * 64 : (q + 1) * 64], pairs)

    part = lax.dynamic_slice(b, (x * 64, 0), (64, BLK))
    part = jnp.concatenate([jnp.where(z == 0, part, 0.0), jnp.where(z == 1, part, 0.0)], 1)
    pack = jnp.concatenate(
        [
            jnp.where(z == core, piece, 0.0),
            jnp.where(core == 0, jnp.where(z == 1, piece, 0.0), part),
        ],
        0,
    )
    pack = jnp.where((y == 0) & (z < 2), pack, 0.0)
    for pairs in LEAD_ROUNDS:
        pack = pack + send(pack, pairs)
    around = []
    for d in (-1, 2, 1):
        around.append(send(pack, shift(dx=d)))
    whole = jnp.stack([pack] + around, 0)
    other = send(whole, SWAP)

    pairs = [(fid(yy, zz, xx, k), fid(yy, 4 * k + xx, zz // 2, zz % 2)) for yy, zz, xx, k in EVERY]
    piece = send(piece, pairs)
    left = send(piece, shift(dz=1))
    right = send(piece, shift(dz=-1))
    three = jnp.stack([left, piece, right], 0)
    left3 = send(three, shift(dz=3))
    right3 = send(three[:2], shift(dz=-3))

    square, stack3, tile2 = (BLK, BLK), (3 * BLK, BLK), (NB, NB)
    first = local(
        first_half0_kernel, [square] * 4, whole, other, scratch=[tile2], flops=FLOPS
    )

    left3, right3 = after(left3, first[0]), after(right3, first[0])
    own = jnp.concatenate([left3, three, right3], 0)
    from_prev = send(own, shift(dy=1))
    from_next = send(own, shift(dy=-1))

    def row_links(pairs):
        return [
            (fid(yy, zz, s, k), fid(yy, zz, d, k))
            for yy in range(NY)
            for zz in range(NZ)
            for k in range(NK)
            for s, d in pairs
        ]

    mine_row = after(jnp.where(x == 0, tile, 0.0), first[0])
    got_row = send(mine_row, row_links(RING4[0]))

    u0, inv0, u01, s11 = local(
        second_half0_kernel, [tile2, tile2, tile2, stack3],
        whole, other, *first, scratch=[tile2, tile2], flops=FLOPS,
    )
    mine_row = mine_row + after(got_row, u0)
    got_row = send(mine_row, row_links(RING4[1]))
    second = local(first_half1_kernel, [square] * 4, s11, flops=FLOPS)
    mine_row = mine_row + after(got_row, second[0])
    other_row = send(mine_row, SWAP)
    from_prev, from_next = after(from_prev, second[0]), after(from_next, second[0])
    far0 = send(from_prev[:4], shift(dy=1))
    far1 = send(from_next[4:], shift(dy=-1))
    u1, inv1 = local(second_half1_kernel, [tile2, tile2], *second, flops=FLOPS)
    other_row, far0, far1 = after(other_row, u1), after(far0, u1), after(far1, u1)
    out, solved = local(
        update_kernel, [a.shape, b.shape],
        whole, other, a, b, mine_row, other_row, own, from_next, far0, far1, from_prev,
        u0, inv0, u01, u1, inv1,
        scratch=[(NY, 2 * NB, NB), tile2], flops=FLOPS,
    )
    return out, solved


FLOPS = 6_000_000_000


def solution(mesh):
    grid = Mesh(mesh.devices.reshape(NY, NZ, NX, NK), AXES)
    rows, cols = ("y", "z"), ("x", "core")
    return jax.shard_map(
        per_device,
        mesh=grid,
        in_specs=(P(rows, cols), P(rows, None)),
        out_specs=(P(rows, cols), P(rows, None)),
        check_vma=False,
    )
```

```python
import jax
import jax.numpy as jnp
from jax import lax
from jax.experimental import pallas as pl
from jax.experimental.pallas import tpu as pltpu
from jax.sharding import Mesh
from jax.sharding import PartitionSpec as P


NB = 256
BLK = 128
SUB = 8
AXES = ("y", "z", "x", "core")
NY, NZ, NX, NK = 4, 8, 4, 2


highest = lax.Precision.HIGHEST


def fid(y, z, x, k):
    return ((y % NY * NZ + z % NZ) * NX + x % NX) * NK + k


EVERY = [
    (y, z, x, k) for y in range(NY) for z in range(NZ) for x in range(NX) for k in range(NK)
]


def shift(dy=0, dz=0, dx=0):
    return [(fid(*p), fid(p[0] + dy, p[1] + dz, p[2] + dx, p[3])) for p in EVERY]


SWAP = [(fid(y, z, x, k), fid(y, z, x, 1 - k)) for y, z, x, k in EVERY]

RING4 = [[(0, 1)], [(0, 3), (1, 2)]]
RING8 = [[(0, 1), (1, 0)], [(0, 6), (1, 3)], [(0, 7), (1, 2), (6, 5), (3, 4)]]


def plane_rounds(order, core):
    have = {"y": [0], "z": [0, 1]}
    rounds = []
    for axis in order:
        for pairs in RING4 if axis == "y" else RING8:
            links = []
            for src, dst in pairs:
                for u in have["z" if axis == "y" else "y"]:
                    for x in range(NX):
                        if axis == "y":
                            links.append((fid(src, u, x, core), fid(dst, u, x, core)))
                        else:
                            links.append((fid(u, src, x, core), fid(u, dst, x, core)))
            have[axis] = sorted(set(have[axis] + [dst for _, dst in pairs]))
            rounds.append(links)
    return rounds


LEAD_ROUNDS = [p + q for p, q in zip(plane_rounds("zy", 0), plane_rounds("yz", 1))]


def send(value, pairs):
    return lax.ppermute(value, AXES, pairs)


def after(value, *others):
    return lax.optimization_barrier((value,) + others)[0]


def eliminate(rows, inv):
    n = len(rows)
    sub = lax.broadcasted_iota(jnp.int32, (SUB, BLK), 0)
    upper, lower_inv = [], []
    for k in range(n):
        D, F = rows[k], inv[k]
        col = [jnp.broadcast_to(D[:, SUB * k + s : SUB * k + s + 1], (SUB, BLK)) for s in range(SUB)]
        recip, cross, d_row, f_row = [], {}, [], []
        scale = jnp.zeros((SUB, BLK), jnp.float32)
        for s in range(SUB):
            pivot = jnp.broadcast_to(col[s][s : s + 1, :], (SUB, BLK))
            recip.append(1.0 / pivot)
            scale = jnp.where(sub == s, lax.rsqrt(pivot), scale)
            mult = jnp.where(sub > s, col[s] * recip[s], 0.0)
            for t in range(s + 1, SUB):
                cross[s, t] = jnp.broadcast_to(col[t][s : s + 1, :], (SUB, BLK))
                col[t] = col[t] - mult * cross[s, t]
            d_row.append(jnp.broadcast_to(D[s : s + 1, :], (SUB, BLK)))
            f_row.append(jnp.broadcast_to(F[s : s + 1, :], (SUB, BLK)))
            if s < SUB - 1:
                D = D - mult * d_row[s]
                F = F - mult * f_row[s]
        upper.append(D * scale)
        lower_inv.append(F * scale)
        for i in range(k + 1, n):
            part = [
                jnp.broadcast_to(rows[i][:, SUB * k + s : SUB * k + s + 1], (SUB, BLK))
                for s in range(SUB)
            ]
            p, q = rows[i], inv[i]
            for s in range(SUB):
                mult = part[s] * recip[s]
                for t in range(s + 1, SUB):
                    part[t] = part[t] - mult * cross[s, t]
                p = p - mult * d_row[s]
                q = q - mult * f_row[s]
            rows[i], inv[i] = p, q
    return upper, lower_inv


def factor_block(block):
    n = BLK // SUB
    rows = [block[SUB * i : SUB * i + SUB, :] for i in range(n)]
    r = lax.broadcasted_iota(jnp.int32, (SUB, BLK), 0)
    c = lax.broadcasted_iota(jnp.int32, (SUB, BLK), 1)
    inv = [jnp.where(r + SUB * i == c, 1.0, 0.0).astype(jnp.float32) for i in range(n)]
    upper, lower_inv = eliminate(rows, inv)
    upper = [jnp.where(c >= r + SUB * i, upper[i], 0.0) for i in range(n)]
    return jnp.concatenate(upper, 0), jnp.concatenate(lower_inv, 0)


def mm(a, b):
    return lax.dot_general(a, b, (((1,), (0,)), ((), ())), precision=highest,
                           preferred_element_type=jnp.float32)


def mm_t(a, b):
    return lax.dot_general(a, b, (((1,), (1,)), ((), ())), precision=highest,
                           preferred_element_type=jnp.float32)


def split(v):
    high = v.astype(jnp.bfloat16)
    return high, (v - high.astype(jnp.float32)).astype(jnp.bfloat16)


def dot3(a, b, transposed=False):
    lhs = jnp.concatenate([a[0], a[0], a[1]], 1)
    rhs = jnp.concatenate([b[0], b[1], b[0]], 1 if transposed else 0)
    dims = (((1,), (1 if transposed else 0,)), ((), ()))
    return lax.dot_general(lhs, rhs, dims, preferred_element_type=jnp.float32)


def position():
    y, z, x, core = (lax.axis_index(n) for n in AXES)
    return y, z, x, core


def unpack(mine_ref, other_ref, rows, plane, out_ref):
    _, _, x, core = position()
    size = rows.stop - rows.start
    for p in range(NX):
        at = lax.rem(p - x + NX, NX)
        mine, other = mine_ref[at, rows], other_ref[at, rows]
        out_ref[p * size : (p + 1) * size] = jnp.where(core == plane, mine, other)


UPPER, LOWER = slice(0, 64), slice(64, 128)


def first_half0_kernel(mine_ref, other_ref, ua_ref, la_ref, ub_ref, s_ref, tile_ref):
    unpack(mine_ref, other_ref, UPPER, 0, tile_ref)
    blocks = (tile_ref[:BLK, :BLK], tile_ref[:BLK, BLK:], tile_ref[BLK:, BLK:])
    first_half(blocks, ua_ref, la_ref, ub_ref, s_ref)


def first_half1_kernel(s_ref, ua_ref, la_ref, ub_ref, out_ref):
    first_half((s_ref[:BLK], s_ref[BLK : 2 * BLK], s_ref[2 * BLK :]), ua_ref, la_ref, ub_ref, out_ref)


def first_half(blocks, ua_ref, la_ref, ub_ref, s_ref):
    ua, la = factor_block(blocks[0])
    ub = mm(la, blocks[1])
    ua_ref[...] = ua
    la_ref[...] = la
    ub_ref[...] = ub
    s_ref[...] = blocks[2] - mm(ub.T, ub)


def second_half(ua, la, ub, s, u_ref, inv_ref):
    uc, lc = factor_block(s)
    zero = jnp.zeros((BLK, BLK), jnp.float32)
    u_ref[:BLK, :BLK] = ua
    u_ref[:BLK, BLK:] = ub
    u_ref[BLK:, :BLK] = zero
    u_ref[BLK:, BLK:] = uc
    inv_ref[:BLK, :BLK] = la
    inv_ref[:BLK, BLK:] = zero
    inv_ref[BLK:, :BLK] = -mm(lc, mm(ub.T, la))
    inv_ref[BLK:, BLK:] = lc


def second_half0_kernel(
    mine_ref, other_ref, ua_ref, la_ref, ub_ref, s_ref,
    u_ref, inv_ref, u01_ref, s11_ref, a10_ref, a11_ref,
):
    unpack(mine_ref, other_ref, LOWER, 0, a10_ref)
    unpack(mine_ref, other_ref, UPPER, 1, a11_ref)
    second_half(ua_ref[...], la_ref[...], ub_ref[...], s_ref[...], u_ref, inv_ref)
    u01_ref[...] = mm_t(inv_ref[...], a10_ref[...])
    left, right = u01_ref[:, :BLK], u01_ref[:, BLK:]
    left_t, right_t = left.T, right.T
    s11_ref[:BLK] = a11_ref[:BLK, :BLK] - mm(left_t, left)
    s11_ref[BLK : 2 * BLK] = a11_ref[:BLK, BLK:] - mm(left_t, right)
    s11_ref[2 * BLK :] = a11_ref[BLK:, BLK:] - mm(right_t, right)


def second_half1_kernel(ua_ref, la_ref, ub_ref, s_ref, u_ref, inv_ref):
    second_half(ua_ref[...], la_ref[...], ub_ref[...], s_ref[...], u_ref, inv_ref)


def panel_tile(low_ref, high_ref, tile_ref, s_inv0, s_inv1, s_u01t):
    z = lax.axis_index("z")
    for p in range(NZ):
        dst = pl.ds(pl.multiple_of(lax.rem(p + z + 4, NZ) * 64, 64), 64)
        tile_ref[dst] = low_ref[p] if p < 4 else high_ref[p - 4]
    c0 = split(dot3(s_inv0, split(tile_ref[:NB]), True))
    c1 = split(dot3(s_inv1, split(tile_ref[NB:].T - dot3(s_u01t, c0))))
    return c0, c1


def update_kernel(
    mine_ref, other_ref, a_ref, b_ref, row_ref, other_row_ref, own_ref, next_ref, far0_ref,
    far1_ref, prev_ref, u0_ref, inv0_ref, u01_ref, u1_ref, inv1_ref,
    out_ref, solved_ref, tile_ref, rhs_ref,
):
    y, z, x, core = position()
    row = y * NZ + z
    row0 = jnp.where(core == 0, row_ref[...], other_row_ref[...])
    row1 = jnp.where(core == 0, other_row_ref[...], row_ref[...])
    u01 = u01_ref[...]
    s_inv0, s_inv1 = split(inv0_ref[...]), split(inv1_ref[...])
    s_u01, s_u01t = split(u01), split(u01.T)
    l0 = dot3(split(row0), s_inv0, True)
    s_l0 = split(l0)
    l1 = dot3(split(row1 - dot3(s_l0, s_u01)), s_inv1, True)
    s_l1 = split(l1)
    s_l = tuple(jnp.concatenate([p, q], 1) for p, q in zip(s_l0, s_l1))
    tiles = (
        (0, own_ref, own_ref.at[4:]),
        (1, next_ref, next_ref.at[4:]),
        (3, prev_ref, prev_ref.at[4:]),
        (2, far0_ref, far1_ref),
    )
    for step, low_ref, high_ref in tiles:
        c0, c1 = panel_tile(low_ref, high_ref, tile_ref.at[step], s_inv0, s_inv1, s_u01t)
        slot = lax.rem(y + step, NY)
        lanes = pl.ds(pl.multiple_of(slot * NB, NB), NB)
        c = tuple(jnp.concatenate([p, q], 0) for p, q in zip(c0, c1))
        new = a_ref[:, lanes] - dot3(s_l, c)
        out_ref[:, lanes] = jnp.where(row >= 2, new, 0.0)
    unpack(mine_ref, other_ref, LOWER, 1, rhs_ref)
    y0 = dot3(s_inv0, split(rhs_ref[:, :BLK]))
    s_y0 = split(y0)
    y1 = dot3(s_inv1, split(rhs_ref[:, BLK:] - dot3(s_u01t, s_y0)))
    solved = b_ref[...] - (dot3(s_l0, s_y0) + dot3(s_l1, split(y1)))
    solved_ref[...] = jnp.where(row == 0, y0, jnp.where(row == 1, y1, solved))

    @pl.when((x == 0) & (core == 0))
    def _():
        out_ref[:, :NB] = jnp.where(row == 0, u0_ref[...].T, l0)

    @pl.when((x == 0) & (core == 1))
    def _():
        out_ref[:, :NB] = jnp.where(row == 0, 0.0, jnp.where(row == 1, u1_ref[...].T, l1))


def local(kernel, outs, *args, scratch=(), flops=0, last=False):
    vmem = pl.BlockSpec(memory_space=pltpu.VMEM)
    args = [pltpu.with_memory_space_constraint(v, pltpu.VMEM) for v in args]
    kept = jax.ShapeDtypeStruct if last else pltpu.VMEM
    return pl.pallas_call(
        kernel,
        out_shape=[kept(s, jnp.float32) for s in outs],
        in_specs=[vmem] * len(args),
        out_specs=[vmem] * len(outs),
        scratch_shapes=[pltpu.VMEM(s, jnp.float32) for s in scratch],
        cost_estimate=pl.CostEstimate(flops=flops, transcendentals=0, bytes_accessed=0),
        compiler_params=pltpu.CompilerParams(vmem_limit_bytes=24 << 20),
    )(*args)


def per_device(a, b):
    y, z, x, core = position()
    tile = a[:, :NB]

    piece = jnp.where(x == 0, tile[:64], 0.0)
    for q in range(1, NX):
        pairs = [
            (fid(yy, zz, 0, k), fid(yy, zz, q, k))
            for yy in range(NY)
            for zz in range(NZ)
            for k in range(NK)
        ]
        piece = piece + send(tile[q * 64 : (q + 1) * 64], pairs)

    part = lax.dynamic_slice(b, (x * 64, 0), (64, BLK))
    part = jnp.concatenate([jnp.where(z == 0, part, 0.0), jnp.where(z == 1, part, 0.0)], 1)
    pack = jnp.concatenate(
        [
            jnp.where(z == core, piece, 0.0),
            jnp.where(core == 0, jnp.where(z == 1, piece, 0.0), part),
        ],
        0,
    )
    pack = jnp.where((y == 0) & (z < 2), pack, 0.0)
    for pairs in LEAD_ROUNDS:
        pack = pack + send(pack, pairs)
    around = []
    for d in (-1, 2, 1):
        around.append(send(pack, shift(dx=d)))
    whole = jnp.stack([pack] + around, 0)
    other = send(whole, SWAP)

    pairs = [(fid(yy, zz, xx, k), fid(yy, 4 * k + xx, zz // 2, zz % 2)) for yy, zz, xx, k in EVERY]
    piece = send(piece, pairs)
    left = send(piece, shift(dz=1))
    right = send(piece, shift(dz=-1))
    three = jnp.stack([left, piece, right], 0)
    left3 = send(three, shift(dz=3))
    right3 = send(three[:2], shift(dz=-3))

    square, stack3, tile2 = (BLK, BLK), (3 * BLK, BLK), (NB, NB)
    first = local(
        first_half0_kernel, [square] * 4, whole, other, scratch=[tile2], flops=FLOPS
    )

    left3, right3 = after(left3, first[0]), after(right3, first[0])
    own = jnp.concatenate([left3, three, right3], 0)
    from_prev = send(own, shift(dy=1))
    from_next = send(own, shift(dy=-1))

    def row_links(pairs):
        return [
            (fid(yy, zz, s, k), fid(yy, zz, d, k))
            for yy in range(NY)
            for zz in range(NZ)
            for k in range(NK)
            for s, d in pairs
        ]

    mine_row = after(jnp.where(x == 0, tile, 0.0), first[0])
    got_row = send(mine_row, row_links(RING4[0]))

    u0, inv0, u01, s11 = local(
        second_half0_kernel, [tile2, tile2, tile2, stack3],
        whole, other, *first, scratch=[tile2, tile2], flops=FLOPS,
    )
    mine_row = mine_row + after(got_row, u0)
    got_row = send(mine_row, row_links(RING4[1]))
    second = local(first_half1_kernel, [square] * 4, s11, flops=FLOPS)
    mine_row = mine_row + after(got_row, second[0])
    other_row = send(mine_row, SWAP)
    from_prev, from_next = after(from_prev, second[0]), after(from_next, second[0])
    far0 = send(from_prev[:4], shift(dy=1))
    far1 = send(from_next[4:], shift(dy=-1))
    u1, inv1 = local(second_half1_kernel, [tile2, tile2], *second, flops=FLOPS)
    other_row, far0, far1 = after(other_row, u1), after(far0, u1), after(far1, u1)
    out, solved = local(
        update_kernel, [a.shape, b.shape],
        whole, other, a, b, mine_row, other_row, own, from_next, far0, far1, from_prev,
        u0, inv0, u01, u1, inv1,
        scratch=[(NY, 2 * NB, NB), tile2], flops=FLOPS, last=True,
    )
    return out, solved


FLOPS = 6_000_000_000


def solution(mesh):
    grid = Mesh(mesh.devices.reshape(NY, NZ, NX, NK), AXES)
    rows, cols = ("y", "z"), ("x", "core")
    return jax.shard_map(
        per_device,
        mesh=grid,
        in_specs=(P(rows, cols), P(rows, None)),
        out_specs=(P(rows, cols), P(rows, None)),
        check_vma=False,
    )
```
